32 devices in a mesh: tm: 4 (over z), chan: 8 (over y, x, core).
Axes of the slice: x: 2, y: 2, z: 4, core: 2. Of those that a mesh axis runs over, the one named last changes fastest.
Arguments:
- voltages: bfloat16 [512, 1024, 1024], P('chan', None, 'tm'), may hold values from -4 to 4
- exponents: int32 [512, 16, 4], P('chan', None, 'tm'), may hold values from -2 to 2
- gain_real: float32 [512, 1024], P(None, 'chan'), may hold values from 0.1 to 1.9
- gain_imag: float32 [512, 1024], P(None, 'chan'), may hold values from -1.5 to 1.5
- delays: float32 [512, 256], replicated, may hold values from -8 to 8
- filter_taps: float32 [4, 1024], replicated, may hold values from -3 to 3
Outputs:
- beam_series: bfloat16 [256, 1024, 1024], P('chan', None, 'tm')
The draws below stay inside these ranges and needn't reach their ends.
All inputs are finite; a program needn't handle non-finite values.
Results may differ from the reference program's by a relative error of at most 0.0062.
Values may be sent and summed in bfloat16 or wider, within the bound.
A program may use at most 320 MiB of HBM per device.

```python
import math
import jax
import jax.numpy as jnp
from jax import lax

S = 512
C = 1024
B = 256
TAPS = 4
CB = 64
F_DEV = 128
GROUPS = 4
NF = 512
SCALE_BLOCKS = 16
N_TM = 4


def set_ends(result, rng, low, high):
    spot = [jax.random.randint(jax.random.fold_in(rng, axis), (), 0, length) for axis, length in enumerate(result.shape)]
    longest = result.shape.index(max(result.shape))
    next_to = spot[:longest] + [(spot[longest] + 1) % result.shape[longest]] + spot[longest + 1:]
    return result.at[tuple(spot)].set(low).at[tuple(next_to)].set(high)


def steps_of(rng, dims, cuts, low, top_value):
    loudness, own = 1.0, jax.random.fold_in(rng, 6)
    for dim, shards_of in cuts:
        heights = jnp.exp(jax.random.uniform(jax.random.fold_in(own, dim), (shards_of,), jnp.float32, low / len(cuts), top_value / len(cuts)))
        loudness = loudness * jnp.repeat(heights, dims[dim] // shards_of).reshape([-1 if axis == dim else 1 for axis in range(len(dims))])
    return loudness


def scatter_about(rng, dims, deviation, bound, split=(), kind=jnp.bfloat16):
    drawn = deviation * jax.random.normal(rng, dims, jnp.float32)
    if split:
        drawn = drawn * steps_of(rng, dims, split, -0.22, 0.18)
    return jnp.clip(drawn, -bound, bound).astype(kind)


def setup_inputs(seed: int = 0) -> dict:
    seeds = jax.random.split(jax.random.key(seed), 7)
    return {
        "voltages": scatter_about(seeds[0], (S, C, 2 * NF), 1.0, 4.0, ((0, 8), (2, 4))),
        "exponents": set_ends(jax.random.randint(seeds[1], (S, SCALE_BLOCKS, GROUPS), -2, 3), jax.random.fold_in(seeds[1], 1), -2, 2).astype(jnp.int32),
        "gain_real": jnp.clip(1.0 + 0.18 * jax.random.normal(seeds[2], (S, C), jnp.float32), 0.1, 1.9),
        "gain_imag": scatter_about(seeds[3], (S, C), 0.3, 1.5, ((1, 8),), jnp.float32),
        "delays": jnp.clip(jax.random.uniform(seeds[4], (S, B), jnp.float32, -8.0, 8.0), -8.0, 8.0),
        "filter_taps": scatter_about(seeds[5], (TAPS, C), 0.5, 3.0, (), jnp.float32),
    }


TWO_PI = 6.283185307179586

def inverse_tables(length):
    row_index = lax.broadcasted_iota(jnp.int32, (length, length), 0)
    col_index = lax.broadcasted_iota(jnp.int32, (length, length), 1)
    phases = TWO_PI / length * (row_index * col_index % length).astype(jnp.float32)
    normalizer = 1.0 / math.sqrt(length)
    cosine_table = (jnp.cos(phases) * normalizer).astype(jnp.bfloat16)
    sine_table = (jnp.sin(phases) * normalizer).astype(jnp.bfloat16)
    return (cosine_table, sine_table)

def reference(voltages, exponents, gain_real, gain_imag, delays, filter_taps):
    stations = voltages.shape[0]
    beam_count = delays.shape[1]
    scale_factor = 1.0 / math.sqrt(stations)
    cosine_table, sine_table = inverse_tables(C)

    def one_channel(channel_index):
        samples = lax.dynamic_index_in_dim(voltages, channel_index, 1, keepdims=False)
        exponent_row = lax.dynamic_index_in_dim(exponents, channel_index // CB, 1, keepdims=False)
        factor = jnp.exp2(exponent_row.astype(jnp.float32)).astype(jnp.bfloat16)
        scaled = (samples.reshape(stations, N_TM, 2 * F_DEV) * factor[:, :, None]).reshape(stations, 2 * NF)
        frequency = (channel_index.astype(jnp.float32) + 0.5) / C - 0.5
        phases = TWO_PI * frequency * jnp.transpose(delays)
        cosines = jnp.cos(phases)
        sines = jnp.sin(phases)
        real_gain = lax.dynamic_index_in_dim(gain_real, channel_index, 1, keepdims=False)[None, :]
        imag_gain = lax.dynamic_index_in_dim(gain_imag, channel_index, 1, keepdims=False)[None, :]
        weight_real = (real_gain * cosines + imag_gain * sines) * scale_factor
        weight_imag = (imag_gain * cosines - real_gain * sines) * scale_factor
        weights = jnp.concatenate([weight_real, weight_imag], axis=0).astype(jnp.bfloat16)
        product = jnp.dot(weights, scaled, preferred_element_type=jnp.float32).reshape(2 * beam_count, N_TM, 2, F_DEV)
        real_part = product[:beam_count, :, 0] - product[beam_count:, :, 1]
        imag_part = product[:beam_count, :, 1] + product[beam_count:, :, 0]
        return jnp.stack([real_part, imag_part], axis=2).astype(jnp.bfloat16)
    beams = lax.map(one_channel, jnp.arange(C, dtype=jnp.int32))
    tail_length = filter_taps.shape[0] - 1

    def one_beam(beam_index):
        spectra = lax.dynamic_index_in_dim(beams, beam_index, 1, keepdims=False).reshape(C, 2 * NF)
        cosine_part = jnp.dot(jnp.transpose(cosine_table), spectra, preferred_element_type=jnp.float32).reshape(C, N_TM, 2, F_DEV)
        sine_part = jnp.dot(jnp.transpose(sine_table), spectra, preferred_element_type=jnp.float32).reshape(C, N_TM, 2, F_DEV)
        real_part = cosine_part[:, :, 0] - sine_part[:, :, 1]
        imag_part = sine_part[:, :, 0] + cosine_part[:, :, 1]
        signal = jnp.stack([real_part, imag_part], axis=1).reshape(C, 2, NF)
        extended = jnp.concatenate([jnp.zeros((C, 2, tail_length), jnp.float32), signal], axis=2)
        running = jnp.zeros((C, 2, NF), jnp.float32)
        for tap_index in range(filter_taps.shape[0]):
            begin = tail_length - tap_index
            running = running + filter_taps[tap_index][:, None, None] * extended[:, :, begin:begin + NF]
        packed = jnp.transpose(running.reshape(C, 2, N_TM, F_DEV), (0, 2, 1, 3)).reshape(C, 2 * NF)
        return packed.astype(jnp.bfloat16)
    return lax.map(one_beam, jnp.arange(beam_count, dtype=jnp.int32))
```

```python
import functools
import math

import jax
import jax.numpy as jnp
from jax import lax
from jax.experimental import pallas as pl
from jax.experimental.pallas import tpu as pltpu
from jax.sharding import PartitionSpec as P


TWO_PI = 6.283185307179586
CHUNKS = 2
VMEM_LIMIT = 56 * 1024 * 1024


def radix_of(chunk_channels):
    return max(r for r in (4, 2, 1) if chunk_channels % r == 0 and (chunk_channels // r) % 16 == 0 or r == 1)


def synthesis_tables(channels, devices, chunk_channels, radix):
    span = channels // radix
    per = chunk_channels // radix
    local = CHUNKS * chunk_channels
    shape = (radix, span, span)
    residue = lax.broadcasted_iota(jnp.int32, shape, 0)
    sample = lax.broadcasted_iota(jnp.int32, shape, 1)
    place = lax.broadcasted_iota(jnp.int32, shape, 2)
    chunk = place // (devices * per)
    source = place // per % devices
    channel = source * local + chunk * chunk_channels + place % per * radix + residue
    phases = TWO_PI / channels * (channel * sample % channels).astype(jnp.float32)
    normalizer = 1.0 / math.sqrt(channels)
    cosine = (jnp.cos(phases) * normalizer).astype(jnp.bfloat16)
    sine = (jnp.sin(phases) * normalizer).astype(jnp.bfloat16)
    return jnp.concatenate([cosine, sine], axis=2)


def beam_weights(gain_real, gain_imag, delays, chan_start, channels):
    local_count = gain_real.shape[1]
    stations = delays.shape[0]
    channel = (chan_start + lax.broadcasted_iota(jnp.int32, (local_count,), 0)).astype(jnp.float32)
    frequency = (channel + 0.5) / channels - 0.5
    turns = TWO_PI * frequency
    phases = turns[:, None, None] * jnp.transpose(delays)[None, :, :]
    cosines = jnp.cos(phases)
    sines = jnp.sin(phases)
    real_gain = jnp.transpose(gain_real)[:, None, :]
    imag_gain = jnp.transpose(gain_imag)[:, None, :]
    scale_factor = 1.0 / math.sqrt(stations)
    weight_real = (real_gain * cosines + imag_gain * sines) * scale_factor
    weight_imag = (imag_gain * cosines - real_gain * sines) * scale_factor
    return weight_real.astype(jnp.bfloat16), weight_imag.astype(jnp.bfloat16)


def beam_kernel(n_taps, wr, wi, x, o, s_re, s_im, ends):
    devices, group, per_device, lanes = x.shape
    beams_local, per = o.shape[1] - 1, o.shape[2]
    beams = devices * beams_local
    half = lanes // 2
    tail = n_taps - 1
    step = pl.program_id(1)
    for j in range(group):
        block = x[:, j].reshape(devices * per_device, lanes)
        real = jnp.dot(wr[j], block, preferred_element_type=jnp.float32)
        imag = jnp.dot(wi[j], block, preferred_element_type=jnp.float32)
        rows = pl.ds(step * group + j, beams, stride=per)
        s_re[rows, :] = real[:, :half] - imag[:, half:]
        s_im[rows, :] = real[:, half:] + imag[:, :half]

    @pl.when(step == pl.num_programs(1) - 1)
    def _():
        take = math.gcd(16, beams_local)
        lane = lax.broadcasted_iota(jnp.int32, (per, half), 1)
        ends[...] = jnp.zeros_like(ends)

        def flush(i, carry):
            device = i * take // beams_local
            base = i * take % beams_local
            src = pl.ds(pl.multiple_of(i * take * per, take * per), take * per)
            for part, scratch in enumerate((s_re, s_im)):
                cols = slice(part * half, (part + 1) * half)
                found = scratch[src, :]
                o[device, pl.ds(base, take), :, cols] = found.reshape(take, per, half).astype(o.dtype)
                total = ends[device, :, cols]
                for t in range(take):
                    place = lane - n_taps * (base + t)
                    moved = pltpu.roll(found[t * per : (t + 1) * per], (n_taps * (base + t) + tail) % half, 1)
                    total = jnp.where(jnp.logical_and(place >= 0, place < tail), moved, total)
                ends[device, :, cols] = total
            return carry

        lax.fori_loop(0, beams // take, flush, 0)
        o[:, beams_local] = ends[...].astype(o.dtype)


def form_beams(weight_real, weight_imag, received, radix, n_taps):
    devices, chunk_channels, per_device, lanes = received.shape
    beams, stations = weight_real.shape[1:]
    per = chunk_channels // radix
    rooms = beams // devices + 1
    group = 4
    view = (per, radix, beams, stations)
    weight_spec = pl.BlockSpec((group, None, beams, stations), lambda r, i: (i, r, 0, 0))
    flops = 8 * chunk_channels * beams * stations * lanes // 2
    return pl.pallas_call(
        functools.partial(beam_kernel, n_taps),
        name="form_beams",
        grid=(radix, per // group),
        in_specs=[
            weight_spec,
            weight_spec,
            pl.BlockSpec((devices, group, None, per_device, lanes), lambda r, i: (0, i, r, 0, 0)),
        ],
        out_specs=pl.BlockSpec((devices, rooms, per, lanes), lambda r, i: (0, 0, r, 0)),
        out_shape=jax.ShapeDtypeStruct((devices, rooms, chunk_channels, lanes), jnp.bfloat16),
        scratch_shapes=[pltpu.VMEM((beams * per, lanes // 2), jnp.float32)] * 2
        + [pltpu.VMEM((devices, per, lanes), jnp.float32)],
        compiler_params=pltpu.CompilerParams(vmem_limit_bytes=VMEM_LIMIT),
        cost_estimate=pl.CostEstimate(
            flops=flops,
            bytes_accessed=2 * chunk_channels * (2 * beams * stations + stations * lanes + beams * lanes),
            transcendentals=0,
        ),
    )(
        weight_real.reshape(view),
        weight_imag.reshape(view),
        received.reshape(devices, per, radix, per_device, lanes),
    )


def times_unit(value, turn, radix):
    re, im = value
    quarter = turn * (4 // radix) % 4
    return ((re, im), (-im, re), (-re, -im), (im, -re))[quarter]


def combine(values, q):
    radix = len(values)
    re, im = values[0]
    for r in range(1, radix):
        more_re, more_im = times_unit(values[r], r * q, radix)
        re, im = re + more_re, im + more_im
    return re, im


def synthesis_kernel(radix, *refs):
    tab, taps, taps_masked = refs[:3]
    blocks = refs[3 : 3 + CHUNKS]
    halos = refs[3 + CHUNKS : 3 + 2 * CHUNKS]
    o, partial, before = refs[3 + 2 * CHUNKS :]
    n_taps, channels, half = taps.shape
    span = channels // radix
    rows = 16
    beam = pl.program_id(0)

    def transform(chunks, slot, r):
        per = chunks[0].shape[1] // radix
        parts = [c[:, r * per : (r + 1) * per, :].reshape(-1, 2 * half) for c in chunks]
        x = jnp.concatenate(parts, axis=0)
        turned = jnp.concatenate([-x[:, half:], x[:, :half]], axis=1)
        both = jnp.concatenate([x, turned], axis=0)
        partial[slot, r] = jnp.dot(tab[r], both, preferred_element_type=jnp.float32)

    def on_rows(start, slot, store):
        values = []
        for r in range(radix):
            both = partial[slot, r, pl.ds(start, rows), :]
            values.append((both[:, :half], both[:, half:]))
        for q in range(radix):
            store(pl.ds(q * span + start, rows), combine(values, q))

    lane = lax.broadcasted_iota(jnp.int32, (rows, half), 1)

    @pl.when(beam == 0)
    def _():
        for r in range(radix):
            transform(halos, 1, r)
        frame = lane % n_taps

        def store(at, signal):
            for part in range(2):
                total = jnp.zeros((rows, half), jnp.float32)
                for k in range(1, n_taps):
                    back = n_taps - 1 - k
                    moved = pltpu.roll(signal[part], (half - back) % half, 1) if back else signal[part]
                    total = total + jnp.where(frame < k, taps[k, at, :] * moved, 0.0)
                before[at, part * half : (part + 1) * half] = total

        def body(i, carry):
            on_rows(pl.multiple_of(i * rows, rows), 1, store)
            return carry

        lax.fori_loop(0, span // rows, body, 0)

    new, old = beam % 2, (beam + 1) % 2
    shift = (half - n_taps * jnp.maximum(beam - 1, 0)) % half

    def store(at, signal):
        for part in range(2):
            cols = slice(part * half, (part + 1) * half)
            total = taps_masked[0, at, :] * signal[part]
            for k in range(1, n_taps):
                total = total + taps_masked[k, at, :] * pltpu.roll(signal[part], k, 1)
            total = total + jnp.where(lane < n_taps - 1, pltpu.roll(before[at, cols], shift, 1), 0.0)
            o[at, cols] = total.astype(o.dtype)

    for r in range(radix):
        transform(blocks, new, r)
        for start in range(r * span // radix, (r + 1) * span // radix, rows):
            on_rows(start, old, store)


def synthesize(tables, filter_taps, spectra, halos, radix):
    devices, rooms, chunk_channels, lanes = spectra[0].shape
    beams = rooms - 1
    n_taps, channels = filter_taps.shape
    half = lanes // 2
    span = channels // radix
    taps = jnp.broadcast_to(filter_taps[:, :, None], (n_taps, channels, half))
    lane = lax.broadcasted_iota(jnp.int32, taps.shape, 2)
    masked = jnp.where(lane >= lax.broadcasted_iota(jnp.int32, taps.shape, 0), taps, 0.0)
    whole = lambda shape: pl.BlockSpec(shape, lambda b: (0,) * len(shape), pipeline_mode=pl.Buffered(1))
    return pl.pallas_call(
        functools.partial(synthesis_kernel, radix),
        name="synthesize",
        grid=(beams + 1,),
        in_specs=[whole(tables.shape), whole(taps.shape), whole(taps.shape)]
        + [pl.BlockSpec((devices, None, chunk_channels, lanes), lambda b: (0, jnp.minimum(b, beams - 1), 0, 0))] * CHUNKS
        + [whole(halos[0].shape)] * CHUNKS,
        out_specs=pl.BlockSpec((None, channels, lanes), lambda b: (jnp.maximum(b - 1, 0), 0, 0)),
        out_shape=jax.ShapeDtypeStruct((beams, channels, lanes), jnp.bfloat16),
        scratch_shapes=[
            pltpu.VMEM((2, radix, span, lanes), jnp.float32),
            pltpu.VMEM((channels, lanes), jnp.float32),
        ],
        compiler_params=pltpu.CompilerParams(vmem_limit_bytes=VMEM_LIMIT),
    )(tables, taps, masked, *spectra, *halos)


def exchange(block):
    return lax.all_to_all(block, "chan", split_axis=0, concat_axis=0, tiled=True)


def per_device(voltages, exponents, gain_real, gain_imag, delays, filter_taps):
    per_station, channels, lanes = voltages.shape
    devices = lax.axis_size("chan")
    local_count = channels // devices
    chunk_channels = local_count // CHUNKS
    radix = radix_of(chunk_channels)
    n_taps = filter_taps.shape[0]
    block_width = channels // exponents.shape[1]
    factor = jnp.repeat(jnp.exp2(exponents.astype(jnp.float32)), block_width, axis=1).astype(jnp.bfloat16)
    factor = factor.reshape(per_station, devices, CHUNKS, chunk_channels, 1)
    start = lax.axis_index("chan") * local_count
    forward = [(i, i + 1) for i in range(lax.axis_size("tm") - 1)]
    received, weights, spectra, halos = [], [], [], []
    source = voltages
    for k in range(CHUNKS):
        parts = source.reshape(per_station, devices, CHUNKS, chunk_channels, lanes)
        packed = jnp.transpose(parts[:, :, k] * factor[:, :, k], (1, 2, 0, 3))
        packed, source = lax.optimization_barrier((packed, source))
        received.append(exchange(packed))
        mine = slice(k * chunk_channels, (k + 1) * chunk_channels)
        first = start + k * chunk_channels
        pair = beam_weights(gain_real[:, mine], gain_imag[:, mine], delays, first, channels)
        held = (pair, delays, gain_real, gain_imag, start)
        pair, delays, gain_real, gain_imag, start = lax.optimization_barrier(held)
        weights.append(pair)
    tables = synthesis_tables(channels, devices, chunk_channels, radix)
    for k in range(CHUNKS):
        beamed = form_beams(*weights[k], received[k], radix, n_taps)
        spectra.append(exchange(beamed))
    for k in range(CHUNKS):
        halos.append(lax.ppermute(spectra[k][:, -1], "tm", forward))
    return synthesize(tables, filter_taps, spectra, halos, radix)


def solution(mesh):
    placed = (
        P("chan", None, "tm"),
        P("chan", None, "tm"),
        P(None, "chan"),
        P(None, "chan"),
        P(),
        P(),
    )

    return jax.shard_map(per_device, mesh=mesh, in_specs=placed, out_specs=P("chan", None, "tm"), check_vma=False)
```

```python
import functools
import math

import jax
import jax.numpy as jnp
from jax import lax
from jax.experimental import pallas as pl
from jax.experimental.pallas import tpu as pltpu
from jax.experimental.layout import Layout, with_layout_constraint
from jax.sharding import PartitionSpec as P


TWO_PI = 6.283185307179586
CHUNKS = 2
VMEM_LIMIT = 56 * 1024 * 1024


def radix_of(chunk_channels):
    return max(r for r in (4, 2, 1) if chunk_channels % r == 0 and (chunk_channels // r) % 16 == 0 or r == 1)


def synthesis_tables(channels, devices, chunk_channels, radix):
    span = channels // radix
    per = chunk_channels // radix
    local = CHUNKS * chunk_channels
    shape = (radix, span, span)
    residue = lax.broadcasted_iota(jnp.int32, shape, 0)
    sample = lax.broadcasted_iota(jnp.int32, shape, 1)
    place = lax.broadcasted_iota(jnp.int32, shape, 2)
    chunk = place // (devices * per)
    source = place // per % devices
    channel = source * local + chunk * chunk_channels + place % per * radix + residue
    phases = TWO_PI / channels * (channel * sample % channels).astype(jnp.float32)
    normalizer = 1.0 / math.sqrt(channels)
    cosine = (jnp.cos(phases) * normalizer).astype(jnp.bfloat16)
    sine = (jnp.sin(phases) * normalizer).astype(jnp.bfloat16)
    return jnp.concatenate([cosine, sine], axis=2)


def beam_weights(gain_real, gain_imag, delays, chan_start, channels):
    local_count = gain_real.shape[1]
    stations = delays.shape[0]
    channel = (chan_start + lax.broadcasted_iota(jnp.int32, (local_count,), 0)).astype(jnp.float32)
    frequency = (channel + 0.5) / channels - 0.5
    turns = TWO_PI * frequency
    phases = turns[:, None, None] * jnp.transpose(delays)[None, :, :]
    cosines = jnp.cos(phases)
    sines = jnp.sin(phases)
    real_gain = jnp.transpose(gain_real)[:, None, :]
    imag_gain = jnp.transpose(gain_imag)[:, None, :]
    scale_factor = 1.0 / math.sqrt(stations)
    weight_real = (real_gain * cosines + imag_gain * sines) * scale_factor
    weight_imag = (imag_gain * cosines - real_gain * sines) * scale_factor
    return weight_real.astype(jnp.bfloat16), weight_imag.astype(jnp.bfloat16)


def beam_kernel(n_taps, wr, wi, x, o, s_re, s_im, ends):
    devices, group, per_device, lanes = x.shape
    beams_local, per = o.shape[1] - 1, o.shape[2]
    beams = devices * beams_local
    half = lanes // 2
    tail = n_taps - 1
    step = pl.program_id(1)
    for j in range(group):
        block = x[:, j].reshape(devices * per_device, lanes)
        real = jnp.dot(wr[j], block, preferred_element_type=jnp.float32)
        imag = jnp.dot(wi[j], block, preferred_element_type=jnp.float32)
        rows = pl.ds(step * group + j, beams, stride=per)
        s_re[rows, :] = real[:, :half] - imag[:, half:]
        s_im[rows, :] = real[:, half:] + imag[:, :half]

    @pl.when(step == pl.num_programs(1) - 1)
    def _():
        take = math.gcd(16, beams_local)
        lane = lax.broadcasted_iota(jnp.int32, (per, half), 1)
        ends[...] = jnp.zeros_like(ends)

        def flush(i, carry):
            device = i * take // beams_local
            base = i * take % beams_local
            src = pl.ds(pl.multiple_of(i * take * per, take * per), take * per)
            for part, scratch in enumerate((s_re, s_im)):
                cols = slice(part * half, (part + 1) * half)
                found = scratch[src, :]
                o[device, pl.ds(base, take), :, cols] = found.reshape(take, per, half).astype(o.dtype)
                total = ends[device, :, cols]
                for t in range(take):
                    place = lane - n_taps * (base + t)
                    moved = pltpu.roll(found[t * per : (t + 1) * per], (n_taps * (base + t) + tail) % half, 1)
                    total = jnp.where(jnp.logical_and(place >= 0, place < tail), moved, total)
                ends[device, :, cols] = total
            return carry

        lax.fori_loop(0, beams // take, flush, 0)
        o[:, beams_local] = ends[...].astype(o.dtype)


def form_beams(weight_real, weight_imag, received, radix, n_taps):
    devices, chunk_channels, per_device, lanes = received.shape
    beams, stations = weight_real.shape[1:]
    per = chunk_channels // radix
    rooms = beams // devices + 1
    group = 4
    view = (per, radix, beams, stations)
    weight_spec = pl.BlockSpec((group, None, beams, stations), lambda r, i: (i, r, 0, 0))
    flops = 8 * chunk_channels * beams * stations * lanes // 2
    return pl.pallas_call(
        functools.partial(beam_kernel, n_taps),
        name="form_beams",
        grid=(radix, per // group),
        in_specs=[
            weight_spec,
            weight_spec,
            pl.BlockSpec((devices, group, None, per_device, lanes), lambda r, i: (0, i, r, 0, 0)),
        ],
        out_specs=pl.BlockSpec((devices, rooms, per, lanes), lambda r, i: (0, 0, r, 0)),
        out_shape=jax.ShapeDtypeStruct((devices, rooms, chunk_channels, lanes), jnp.bfloat16),
        scratch_shapes=[pltpu.VMEM((beams * per, lanes // 2), jnp.float32)] * 2
        + [pltpu.VMEM((devices, per, lanes), jnp.float32)],
        compiler_params=pltpu.CompilerParams(vmem_limit_bytes=VMEM_LIMIT),
        cost_estimate=pl.CostEstimate(
            flops=flops,
            bytes_accessed=2 * chunk_channels * (2 * beams * stations + stations * lanes + beams * lanes),
            transcendentals=0,
        ),
    )(
        weight_real.reshape(view),
        weight_imag.reshape(view),
        received.reshape(devices, per, radix, per_device, lanes),
    )


def times_unit(value, turn, radix):
    re, im = value
    quarter = turn * (4 // radix) % 4
    return ((re, im), (-im, re), (-re, -im), (im, -re))[quarter]


def combine(values, q):
    radix = len(values)
    re, im = values[0]
    for r in range(1, radix):
        more_re, more_im = times_unit(values[r], r * q, radix)
        re, im = re + more_re, im + more_im
    return re, im


def synthesis_kernel(radix, *refs):
    tab, taps_masked = refs[:2]
    blocks = refs[2 : 2 + CHUNKS]
    halos = refs[2 + CHUNKS : 2 + 2 * CHUNKS]
    o, partial, before = refs[2 + 2 * CHUNKS :]
    n_taps, channels, half = taps_masked.shape
    span = channels // radix
    rows = 16
    beam = pl.program_id(0)

    def transform(chunks, slot, r):
        per = chunks[0].shape[1] // radix
        parts = [c[:, r * per : (r + 1) * per, :].reshape(-1, 2 * half) for c in chunks]
        x = jnp.concatenate(parts, axis=0)
        turned = jnp.concatenate([-x[:, half:], x[:, :half]], axis=1)
        both = jnp.concatenate([x, turned], axis=0)
        partial[slot, r] = jnp.dot(tab[r], both, preferred_element_type=jnp.float32)

    def on_rows(start, slot, store):
        values = []
        for r in range(radix):
            both = partial[slot, r, pl.ds(start, rows), :]
            values.append((both[:, :half], both[:, half:]))
        for q in range(radix):
            store(pl.ds(q * span + start, rows), combine(values, q))

    lane = lax.broadcasted_iota(jnp.int32, (rows, half), 1)

    @pl.when(beam == 0)
    def _():
        for r in range(radix):
            transform(halos, 1, r)
        frame = lane % n_taps

        def store(at, signal):
            for part in range(2):
                total = jnp.zeros((rows, half), jnp.float32)
                for k in range(1, n_taps):
                    back = n_taps - 1 - k
                    moved = pltpu.roll(signal[part], (half - back) % half, 1) if back else signal[part]
                    tap = jnp.broadcast_to(taps_masked[k, at, :][:, half - 1 :], (rows, half))
                    total = total + jnp.where(frame < k, tap * moved, 0.0)
                before[at, part * half : (part + 1) * half] = total

        def body(i, carry):
            on_rows(pl.multiple_of(i * rows, rows), 1, store)
            return carry

        lax.fori_loop(0, span // rows, body, 0)

    new, old = beam % 2, (beam + 1) % 2
    shift = (half - n_taps * jnp.maximum(beam - 1, 0)) % half

    def store(at, signal):
        for part in range(2):
            cols = slice(part * half, (part + 1) * half)
            total = taps_masked[0, at, :] * signal[part]
            for k in range(1, n_taps):
                total = total + taps_masked[k, at, :] * pltpu.roll(signal[part], k, 1)
            total = total + jnp.where(lane < n_taps - 1, pltpu.roll(before[at, cols], shift, 1), 0.0)
            o[at, cols] = total.astype(o.dtype)

    for r in range(radix):
        transform(blocks, new, r)
        for start in range(r * span // radix, (r + 1) * span // radix, rows):
            on_rows(start, old, store)


def synthesize(tables, filter_taps, spectra, halos, radix):
    devices, rooms, chunk_channels, lanes = spectra[0].shape
    beams = rooms - 1
    n_taps, channels = filter_taps.shape
    half = lanes // 2
    span = channels // radix
    taps = jnp.broadcast_to(filter_taps[:, :, None], (n_taps, channels, half))
    lane = lax.broadcasted_iota(jnp.int32, taps.shape, 2)
    masked = jnp.where(lane >= lax.broadcasted_iota(jnp.int32, taps.shape, 0), taps, 0.0)
    whole = lambda shape: pl.BlockSpec(shape, lambda b: (0,) * len(shape), pipeline_mode=pl.Buffered(1))
    return pl.pallas_call(
        functools.partial(synthesis_kernel, radix),
        name="synthesize",
        grid=(beams + 1,),
        in_specs=[whole(tables.shape), whole(taps.shape)]
        + [pl.BlockSpec((devices, None, chunk_channels, lanes), lambda b: (0, jnp.minimum(b, beams - 1), 0, 0))] * CHUNKS
        + [whole(halos[0].shape)] * CHUNKS,
        out_specs=pl.BlockSpec((None, channels, lanes), lambda b: (jnp.maximum(b - 1, 0), 0, 0)),
        out_shape=jax.ShapeDtypeStruct((beams, channels, lanes), jnp.bfloat16),
        scratch_shapes=[
            pltpu.VMEM((2, radix, span, lanes), jnp.float32),
            pltpu.VMEM((channels, lanes), jnp.float32),
        ],
        compiler_params=pltpu.CompilerParams(vmem_limit_bytes=VMEM_LIMIT),
    )(tables, masked, *spectra, *halos)


def exchange(block):
    return lax.all_to_all(block, "chan", split_axis=0, concat_axis=0, tiled=True)


def per_device(voltages, exponents, gain_real, gain_imag, delays, filter_taps):
    per_station, channels, lanes = voltages.shape
    devices = lax.axis_size("chan")
    local_count = channels // devices
    chunk_channels = local_count // CHUNKS
    radix = radix_of(chunk_channels)
    n_taps = filter_taps.shape[0]
    block_width = channels // exponents.shape[1]
    factor = jnp.repeat(jnp.exp2(exponents.astype(jnp.float32)), block_width, axis=1).astype(jnp.bfloat16)
    factor = factor.reshape(per_station, devices, CHUNKS, chunk_channels, 1)
    start = lax.axis_index("chan") * local_count
    forward = [(i, i + 1) for i in range(lax.axis_size("tm") - 1)]
    received, weights, spectra, halos = [], [], [], []
    source = voltages
    for k in range(CHUNKS):
        parts = source.reshape(per_station, devices, CHUNKS, chunk_channels, lanes)
        packed = jnp.transpose(parts[:, :, k] * factor[:, :, k], (1, 0, 2, 3))
        packed = with_layout_constraint(packed, Layout(major_to_minor=(0, 1, 2, 3)))
        packed, source = lax.optimization_barrier((packed, source))
        landed = with_layout_constraint(exchange(packed), Layout(major_to_minor=(0, 1, 2, 3)))
        received.append(jnp.transpose(landed, (0, 2, 1, 3)))
        mine = slice(k * chunk_channels, (k + 1) * chunk_channels)
        first = start + k * chunk_channels
        pair = beam_weights(gain_real[:, mine], gain_imag[:, mine], delays, first, channels)
        held = (pair, delays, gain_real, gain_imag, start)
        pair, delays, gain_real, gain_imag, start = lax.optimization_barrier(held)
        weights.append(pair)
    tables = synthesis_tables(channels, devices, chunk_channels, radix)
    for k in range(CHUNKS):
        beamed = form_beams(*weights[k], received[k], radix, n_taps)
        spectra.append(exchange(beamed))
    for k in range(CHUNKS):
        halos.append(lax.ppermute(spectra[k][:, -1], "tm", forward))
    return synthesize(tables, filter_taps, spectra, halos, radix)


def solution(mesh):
    placed = (
        P("chan", None, "tm"),
        P("chan", None, "tm"),
        P(None, "chan"),
        P(None, "chan"),
        P(),
        P(),
    )

    return jax.shard_map(per_device, mesh=mesh, in_specs=placed, out_specs=P("chan", None, "tm"), check_vma=False)
```
